32 devices in a mesh: row: 4 (over x, core), col: 4 (over z), vir: 2 (over y).
Axes of the slice: x: 2, y: 2, z: 4, core: 2. Of those that a mesh axis runs over, the one named last changes fastest.
Arguments:
- amplitudes: float32 [80, 4, 4, 3, 128, 128], P('vir', 'row', 'col'), may hold values from -6 to 6
- integrals: float32 [80, 4, 4, 3, 128, 128], P('vir', 'row', 'col'), may hold values from -6 to 6
- cycle_terms: float32 [80, 4, 4, 3, 128, 128], P('vir', 'row', 'col'), may hold values from -0.15625 to 0.15625
- ladder_factors: float32 [80, 8, 128, 128], P('vir'), may hold values from -0.375 to 0.375
- live: int32 [80, 4, 4, 3], P('vir', 'row', 'col'), may hold values 0 or 1
Outputs:
- residual: float32 [80, 4, 4, 3, 128, 128], P('vir', 'row', 'col')
The draws below stay inside these ranges and needn't reach their ends.
All inputs are finite; a program needn't handle non-finite values. No bound on the sum of `live` on one device may be relied on, other than what follows from the above.
Results may differ from the reference program's by a relative error of at most 0.0001.
Values sent between devices are 32-bit elements; how exact they have to be, the bound alone decides.
No kernel may reach another device: no remote copies, remote signals or barrier semaphores. Data moves between devices by JAX's collectives and lax.ppermute only.
A program may use at most 448 MiB of HBM per device.

```python
import jax
import jax.numpy as jnp
from jax import lax

TILE = 128
NT = 80
BAND = 3
NQ = 8
NOCC = 4


def touch_ends(entries, key, least, top_value):
    spot = [jax.random.randint(jax.random.fold_in(key, axis), (), 0, length) for axis, length in enumerate(entries.shape)]
    main_axis = entries.shape.index(max(entries.shape))
    beside = spot[:main_axis] + [(spot[main_axis] + 1) % entries.shape[main_axis]] + spot[main_axis + 1:]
    return entries.at[tuple(spot)].set(least).at[tuple(beside)].set(top_value)


def level_of(key, extent, shards, least, top_value):
    level, own = 1.0, jax.random.fold_in(key, 6)
    for dim, blocks in shards:
        steps = jnp.exp(jax.random.uniform(jax.random.fold_in(own, dim), (blocks,), jnp.float32, least / len(shards), top_value / len(shards)))
        level = level * jnp.repeat(steps, extent[dim] // blocks).reshape([-1 if axis == dim else 1 for axis in range(len(extent))])
    return level


def centred(key, shape, width, bound, split=(), dtype=jnp.bfloat16):
    level = level_of(key, shape, split, -0.22, 0.18) if split else 1.0
    drawn = jax.random.normal(key, shape, jnp.float32) * width * level
    return jnp.minimum(jnp.maximum(drawn, -bound), bound).astype(dtype)


def setup_inputs(seed: int = 0) -> dict:
    arg_keys = jax.random.split(jax.random.key(seed), 6)
    return {
        "amplitudes": centred(arg_keys[0], (NT, NOCC, NOCC, BAND, TILE, TILE), 1.0, 6.0, ((0, 2), (1, 4), (2, 4)), jnp.float32),
        "integrals": centred(arg_keys[1], (NT, NOCC, NOCC, BAND, TILE, TILE), 1.0, 6.0, ((0, 2), (1, 4), (2, 4)), jnp.float32),
        "cycle_terms": centred(arg_keys[2], (NT, NOCC, NOCC, BAND, TILE, TILE), (TILE * NOCC * BAND) ** -0.5, 0.15625, ((0, 2), (1, 4), (2, 4)), jnp.float32),
        "ladder_factors": centred(arg_keys[3], (NT, NQ, TILE, TILE), (TILE * 2) ** -0.5, 0.375, ((0, 2),), jnp.float32),
        "live": touch_ends((jax.random.randint(arg_keys[4], (NT, NOCC, NOCC, BAND), 0, 3) < 2).astype(jnp.int32), jax.random.fold_in(arg_keys[4], 1), 0, 1),
    }


def reference(amplitudes, integrals, cycle_terms, ladder_factors, live):
    half_band = BAND // 2
    slot_index = jnp.arange(BAND)
    tile_rows = jnp.arange(NT)
    col_tile = tile_rows[:, None] + slot_index[None, :] - half_band
    inside = (col_tile >= 0) & (col_tile < NT)
    keep = ((live == 1) | (slot_index == half_band)[None, None, None, :]) & inside[:, None, None, :]
    keep_float = keep.astype(jnp.float32)[..., None, None]
    amps = amplitudes * keep_float
    padded_factors = jnp.pad(ladder_factors, ((half_band, half_band), (0, 0), (0, 0), (0, 0)))
    ladder = jnp.zeros(amplitudes.shape, jnp.float32)
    for term_index in range(NQ):
        inner = jnp.einsum('axy,aijsyz->aijsxz', ladder_factors[:, term_index], amps,
                           precision=lax.Precision.HIGHEST)
        parts = []
        for out_slot in range(BAND):
            right_side = padded_factors[out_slot:out_slot + NT, term_index]
            parts.append(jnp.einsum('aijxz,awz->aijxw', inner[:, :, :, out_slot], right_side,
                                    precision=lax.Precision.HIGHEST))
        ladder = ladder + jnp.stack(parts, axis=3)
    padded_cycle = jnp.pad(cycle_terms, ((half_band, half_band), (0, 0), (0, 0), (0, 0), (0, 0), (0, 0)))
    cycle_slots = []
    for out_slot in range(BAND):
        total = jnp.zeros(amplitudes.shape[:3] + amplitudes.shape[4:], jnp.float32)
        for in_slot in range(BAND):
            mid_slot = out_slot - in_slot + half_band
            if 0 <= mid_slot < BAND:
                cycle_rows = padded_cycle[in_slot:in_slot + NT, :, :, mid_slot]
                total = total + jnp.einsum('aiktu,akjuv->aijtv', amps[:, :, :, in_slot], cycle_rows,
                                           precision=lax.Precision.HIGHEST)
        cycle_slots.append(total)
    cycle = jnp.stack(cycle_slots, axis=3)
    return keep_float * ((integrals + ladder) + cycle)
```

```python
import functools

import jax
import jax.numpy as jnp
from jax import lax
from jax.experimental import pallas as pl
from jax.experimental.pallas import tpu as pltpu
from jax.sharding import PartitionSpec as P


F32 = jnp.float32
BF16 = jnp.bfloat16


def split(x):
    high = x.astype(BF16)
    low = (x - high.astype(F32)).astype(BF16)
    return high, low


def dot(a, b):
    return lax.dot_general(a, b, (((1,), (0,)), ((), ())), preferred_element_type=F32)


def dot_nt(a, b):
    return lax.dot_general(a, b, (((1,), (1,)), ((), ())), preferred_element_type=F32)


def row_chunks(count, parts):
    sizes = [2 * ((count // 2 * (p + 1)) // parts - (count // 2 * p) // parts) for p in range(parts)]
    sizes = [s for s in sizes if s]
    sizes[0] += count - sum(sizes)
    edges, start = [], 0
    for s in sizes:
        edges.append((start, start + s))
        start += s
    return edges


def ladder_body(start, count, keep_ref, amp_ref, int_ref, prev_ref, cur_ref, next_ref, halo_ref, *rest):
    out_ref, high_ref, low_ref = rest[-3:]
    step = pl.program_id(0)
    row = start + step
    terms = cur_ref.shape[1]
    slots = amp_ref.shape[3]
    tile = amp_ref.shape[4]

    def store(slot, ref):
        for q in range(terms):
            high, low = split(ref[0, q])
            high_ref[slot, :, q * tile : (q + 1) * tile] = high
            low_ref[slot, :, q * tile : (q + 1) * tile] = low

    @pl.when(step == 0)
    def _():
        store(lax.rem(row + 2, 3), prev_ref)
        store(lax.rem(row, 3), cur_ref)

    @pl.when(row < count - 1)
    def _():
        store(lax.rem(row + 1, 3), next_ref)

    @pl.when(row == count - 1)
    def _():
        store(lax.rem(row + 1, 3), halo_ref)

    here = lax.rem(row, 3)
    left_high = jnp.concatenate([high_ref[here, :, q * tile : (q + 1) * tile] for q in range(terms)], axis=0)
    left_low = jnp.concatenate([low_ref[here, :, q * tile : (q + 1) * tile] for q in range(terms)], axis=0)
    left_both = jnp.concatenate([left_high, left_low], axis=1)
    for s in range(slots):
        amp_high, amp_low = split(amp_ref[0, 0, 0, s])
        inner = dot(left_both, jnp.concatenate([amp_high, amp_high], axis=0)) + dot(left_high, amp_low)
        inner_high, inner_low = split(inner)
        wide_high = jnp.concatenate([inner_high[q * tile : (q + 1) * tile] for q in range(terms)], axis=1)
        wide_low = jnp.concatenate([inner_low[q * tile : (q + 1) * tile] for q in range(terms)], axis=1)
        there = lax.rem(row + s + 2, 3)
        right_high = high_ref[there]
        both = dot_nt(wide_high, jnp.concatenate([right_high, low_ref[there]], axis=0))
        total = both[:, :tile] + both[:, tile:] + dot_nt(wide_low, right_high)
        out_ref[0, 0, 0, s] = int_ref[0, 0, 0, s] + total


def ladder(buf, keep, amps, integrals, factors, halo_low, halo_high, edge):
    start, stop = edge
    count = integrals.shape[0]
    slots, tile = amps.shape[3], amps.shape[4]
    terms = factors.shape[1]
    block = (1, 1, 1, slots, tile, tile)
    fblock = (1, terms, tile, tile)
    prev = halo_low if start == 0 else factors
    prev_row = 0 if start == 0 else start - 1
    in_specs = [
        pl.BlockSpec(block, lambda g, keep: (g, 0, 0, 0, 0, 0)),
        pl.BlockSpec(block, lambda g, keep: (start + g, 0, 0, 0, 0, 0)),
        pl.BlockSpec(fblock, lambda g, keep: (prev_row, 0, 0, 0)),
        pl.BlockSpec(fblock, lambda g, keep: (start, 0, 0, 0)),
        pl.BlockSpec(fblock, lambda g, keep: (jnp.minimum(start + g + 1, count - 1), 0, 0, 0)),
        pl.BlockSpec(fblock, lambda g, keep: (0, 0, 0, 0)),
    ]
    args = [keep, amps, integrals, prev, factors, factors, halo_high]
    aliases = {}
    if buf is not None:
        in_specs.append(pl.BlockSpec(memory_space=pl.ANY))
        aliases = {len(args): 0}
        args.append(buf)
    rows = stop - start
    return pl.pallas_call(
        functools.partial(ladder_body, start, count),
        out_shape=jax.ShapeDtypeStruct(integrals.shape, F32),
        grid_spec=pltpu.PrefetchScalarGridSpec(
            num_scalar_prefetch=1,
            grid=(rows,),
            in_specs=in_specs,
            out_specs=pl.BlockSpec(block, lambda g, keep: (start + g, 0, 0, 0, 0, 0)),
            scratch_shapes=[
                pltpu.VMEM((3, tile, terms * tile), BF16),
                pltpu.VMEM((3, tile, terms * tile), BF16),
            ],
        ),
        input_output_aliases=aliases,
        cost_estimate=pl.CostEstimate(
            flops=rows * slots * terms * 12 * tile**3,
            transcendentals=0,
            bytes_accessed=rows * (3 * slots + terms) * tile * tile * 4,
        ),
        name="ladder",
    )(*args)


def cycle_sum(amp_tiles, term_high, term_low, slots, tile):
    half = slots // 2
    pieces = [None] * slots
    for t in range(slots):
        first = max(0, half - t)
        last = min(slots, slots + half - t)
        amp_high, amp_low = split(amp_tiles(t))
        high = term_high(t, first, last)
        got = dot(amp_high, high) + dot(amp_high, term_low(t, first, last)) + dot(amp_low, high)
        for m in range(first, last):
            s = t + m - half
            part = got[:, (m - first) * tile : (m - first + 1) * tile]
            pieces[s] = part if pieces[s] is None else pieces[s] + part
    return pieces


def keep_terms(refs, high_ref, low_ref, slot, tile):
    for high_at, value in refs:
        for m in range(value.shape[0]):
            high, low = split(value[m])
            high_ref[slot, high_at, :, m * tile : (m + 1) * tile] = high
            low_ref[slot, high_at, :, m * tile : (m + 1) * tile] = low


def own_body(start, meta_ref, keep_ref, base_ref, own_ref, below_ref, above_ref, far_ref, tail_ref, new_ref, extra_ref,
             out_ref, high_ref, low_ref):
    step = pl.program_id(0)
    row = start + step
    slots, tile = own_ref.shape[3], own_ref.shape[4]
    groups = new_ref.shape[0]

    @pl.when(step == 0)
    def _():
        for b in range(2):
            keep_terms([(k, tail_ref[k, b]) for k in range(groups)], high_ref, low_ref, b, tile)

    keep_terms([(k, new_ref[k, 0]) for k in range(groups)], high_ref, low_ref, lax.rem(step + 2, 3), tile)
    sources = (own_ref, below_ref, above_ref, far_ref)
    index = [meta_ref[j] for j in range(4)]

    def amp_tiles(t):
        return jnp.concatenate([ref[0, 0, 0, t] for ref in sources], axis=1)

    def terms(ref):
        def get(t, first, last):
            slot = lax.rem(step + t, 3)
            return jnp.concatenate([ref[slot, k, :, first * tile : last * tile] for k in index], axis=0)
        return get

    pieces = cycle_sum(amp_tiles, terms(high_ref), terms(low_ref), slots, tile)
    for s in range(slots):
        flag = keep_ref[row * slots + s] != 0
        total = base_ref[0, 0, 0, s] + pieces[s] + extra_ref[0, 0, 0, s]
        out_ref[0, 0, 0, s] = jnp.where(flag, total, 0.0)


def own_cycle(buf, meta, keep, own, below, above, far, prev_terms, new_terms, first, extra, edge):
    start, stop = edge
    rows = stop - start
    slots, tile = own.shape[3], own.shape[4]
    groups = new_terms.shape[0]
    block = (1, 1, 1, slots, tile, tile)
    local = pl.BlockSpec(block, lambda g, *_: (g, 0, 0, 0, 0, 0))
    whole = pl.BlockSpec(block, lambda g, *_: (start + g, 0, 0, 0, 0, 0))
    shift = 2 if first else 0
    tail_at = 0 if first else prev_terms.shape[1] // 2 - 1
    return pl.pallas_call(
        functools.partial(own_body, start),
        out_shape=jax.ShapeDtypeStruct(buf.shape, F32),
        grid_spec=pltpu.PrefetchScalarGridSpec(
            num_scalar_prefetch=2,
            grid=(rows,),
            in_specs=[
                whole, local, local, local, local,
                pl.BlockSpec((groups, 2, slots, tile, tile), lambda g, *_: (0, tail_at, 0, 0, 0)),
                pl.BlockSpec((groups, 1, slots, tile, tile), lambda g, *_: (0, g + shift, 0, 0, 0)),
                local,
            ],
            out_specs=whole,
            scratch_shapes=[
                pltpu.VMEM((3, groups, tile, slots * tile), BF16),
                pltpu.VMEM((3, groups, tile, slots * tile), BF16),
            ],
        ),
        input_output_aliases={2: 0},
        cost_estimate=pl.CostEstimate(
            flops=rows * 7 * 4 * 6 * tile**3,
            transcendentals=0,
            bytes_accessed=rows * slots * 11 * tile * tile * 4,
        ),
        name="own_cycle",
    )(meta, keep, buf, own, below, above, far, prev_terms, new_terms, extra)


def far_body(meta_ref, below_ref, above_ref, far_ref, tail0_ref, tail1_ref, new0_ref, new1_ref,
             out_ref, high_ref, low_ref):
    step = pl.program_id(0)
    slots, tile = far_ref.shape[3], far_ref.shape[4]
    active, use_below, parity, near_slot, far_slot = (meta_ref[4 + j] for j in range(5))

    @pl.when(active != 0)
    def _():
        @pl.when(step == 0)
        def _():
            for b in range(2):
                keep_terms([(parity, tail0_ref[b]), (1 - parity, tail1_ref[b])], high_ref, low_ref, b, tile)

        keep_terms([(parity, new0_ref[0]), (1 - parity, new1_ref[0])], high_ref, low_ref, lax.rem(step + 2, 3), tile)

        def amp_tiles(t):
            near = jnp.where(use_below != 0, below_ref[0, 0, 0, t], above_ref[0, 0, 0, t])
            return jnp.concatenate([near, far_ref[0, 0, 0, t]], axis=1)

        def terms(ref):
            def get(t, first, last):
                slot = lax.rem(step + t, 3)
                return jnp.concatenate(
                    [ref[slot, k, :, first * tile : last * tile] for k in (near_slot, far_slot)], axis=0
                )
            return get

        pieces = cycle_sum(amp_tiles, terms(high_ref), terms(low_ref), slots, tile)
        for s in range(slots):
            out_ref[0, 0, 0, s] = pieces[s]

    @pl.when(active == 0)
    def _():
        out_ref[...] = jnp.zeros_like(out_ref)


def far_cycle(meta, below, above, far, prev0, prev1, new0, new1, first):
    rows, slots, tile = far.shape[0], far.shape[3], far.shape[4]
    block = (1, 1, 1, slots, tile, tile)
    local = pl.BlockSpec(block, lambda g, *_: (g, 0, 0, 0, 0, 0))
    shift = 2 if first else 0
    tail_at = 0 if first else prev0.shape[0] // 2 - 1
    tail = pl.BlockSpec((2, slots, tile, tile), lambda g, *_: (tail_at, 0, 0, 0))
    new = pl.BlockSpec((1, slots, tile, tile), lambda g, *_: (g + shift, 0, 0, 0))
    return pl.pallas_call(
        far_body,
        out_shape=jax.ShapeDtypeStruct(far.shape, F32),
        grid_spec=pltpu.PrefetchScalarGridSpec(
            num_scalar_prefetch=1,
            grid=(rows,),
            in_specs=[local, local, local, tail, tail, new, new],
            out_specs=local,
            scratch_shapes=[
                pltpu.VMEM((3, 2, tile, slots * tile), BF16),
                pltpu.VMEM((3, 2, tile, slots * tile), BF16),
            ],
        ),
        cost_estimate=pl.CostEstimate(
            flops=rows * 7 * 2 * 6 * tile**3,
            transcendentals=0,
            bytes_accessed=rows * slots * 6 * tile * tile * 4,
        ),
        name="far_cycle",
    )(meta, below, above, far, prev0, prev1, new0, new1)


def tie(value, *others):
    return lax.optimization_barrier((value, *others))[0]


def per_device(total_tiles, parts, ahead, amplitudes, integrals, cycle_terms, ladder_factors, live):
    count, _, _, slots, tile, _ = amplitudes.shape
    half = slots // 2
    col, row, vir = lax.axis_index("col"), lax.axis_index("row"), lax.axis_index("vir")
    virs = lax.axis_size("vir")
    edges = row_chunks(count, parts)
    chunks = len(edges)

    slot_index = jnp.arange(slots)
    col_tile = (vir * count + jnp.arange(count))[:, None] + slot_index[None, :] - half
    inside = (col_tile >= 0) & (col_tile < total_tiles)
    keep = ((live.reshape(count, slots) == 1) | (slot_index == half)[None, :]) & inside
    flags = keep.astype(jnp.int32).reshape(-1)
    keep_float = keep.astype(F32).reshape(count, 1, 1, slots, 1, 1)

    middle_high = col == 2
    far_k = jnp.where(middle_high, 0, 3)
    near_k = jnp.where(middle_high, 1, 2)
    meta = jnp.stack([
        col, jnp.maximum(col - 1, 0), jnp.minimum(col + 1, 3), far_k,
        ((col == 1) | (col == 2)).astype(jnp.int32), middle_high.astype(jnp.int32),
        row % 2, near_k % 2, far_k % 2,
    ]).astype(jnp.int32)

    up = [(i, i + 1) for i in range(virs - 1)]
    down = [(i + 1, i) for i in range(virs - 1)]
    terms3 = cycle_terms.reshape(count, slots, tile, tile)
    term_low = lax.ppermute(terms3[count - 1 :], "vir", up)
    term_high = lax.ppermute(terms3[:1], "vir", down)
    factor_low = lax.ppermute(ladder_factors[count - 1 :], "vir", up)
    factor_high = lax.ppermute(ladder_factors[:1], "vir", down)

    own, below, above, far, gathered, far0, far1, partial, extra = ([None] * chunks for _ in range(9))
    for c, (lo, hi) in enumerate(edges):
        mine = amplitudes[lo:hi] * keep_float[lo:hi]
        if c >= ahead:
            mine = tie(mine, below[c - ahead], above[c - ahead])
        own[c] = mine
        below[c] = lax.ppermute(mine, "col", [(0, 1), (1, 2), (2, 3)])
        above[c] = lax.ppermute(mine, "col", [(1, 0), (2, 1), (3, 2)])

    for c, (lo, hi) in enumerate(edges):
        rows = [terms3[lo + 1 if c else 0 : min(hi + 1, count)]]
        if c == 0:
            rows.insert(0, term_low)
        if c == chunks - 1:
            rows.append(term_high)
        gathered[c] = lax.all_gather(jnp.concatenate(rows, axis=0), "row")

    buf = None
    for c, edge in enumerate(edges):
        buf = ladder(buf, flags, own[c], integrals, ladder_factors, factor_low, factor_high, edge)

    send_k = jnp.where(col == 3, 0, 2) + row % 2
    for c, edge in enumerate(edges):
        first = c == 0
        prev = 0 if first else c - 1
        far[c] = lax.ppermute(jnp.where(col == 1, below[c], above[c]), "col", [(1, 2), (2, 1)])
        chosen = lax.dynamic_index_in_dim(gathered[c], send_k, 0, keepdims=False)
        far0[c] = lax.ppermute(chosen, "col", [(3, 2), (0, 1)])
        far1[c] = lax.ppermute(far0[c], "row", [(i, i ^ 1) for i in range(4)])
        partial[c] = far_cycle(meta, below[c], above[c], far[c], far0[prev], far1[prev], far0[c], far1[c], first)
        extra[c] = lax.ppermute(partial[c], "col", [(2, 3), (1, 0)])
    for c, edge in enumerate(edges):
        first = c == 0
        prev = 0 if first else c - 1
        buf = own_cycle(buf, meta, flags, own[c], below[c], above[c], far[c], gathered[prev], gathered[c], first,
                        extra[c], edge)
    return buf


def extended(block, sides, width):
    for axis, dim in sides:
        count = lax.axis_size(axis)
        forward = [(i, i + 1) for i in range(count - 1)]
        backward = [(target, source) for source, target in forward]
        low = lax.ppermute(
            lax.slice_in_dim(block, block.shape[dim] - width, None, axis=dim), axis, forward
        )
        high = lax.ppermute(lax.slice_in_dim(block, 0, width, axis=dim), axis, backward)
        block = jnp.concatenate([low, block, high], axis=dim)
    return block


def general(total_tiles, amplitudes, integrals, cycle_terms, ladder_factors, live):
    count, occupied, _, slots, tile, _ = amplitudes.shape
    terms = ladder_factors.shape[1]
    half = slots // 2
    slot_index = jnp.arange(slots)
    global_rows = lax.axis_index("vir") * count + jnp.arange(count)
    col_tile = global_rows[:, None] + slot_index[None, :] - half
    inside = (col_tile >= 0) & (col_tile < total_tiles)
    keep = ((live == 1) | (slot_index == half)[None, None, None, :]) & inside[:, None, None, :]
    keep_float = keep.astype(F32)[..., None, None]
    amps = amplitudes * keep_float
    cycle_all = lax.all_gather(extended(cycle_terms, (("vir", 0),), half), "row", axis=1, tiled=True)
    factors = extended(ladder_factors, (("vir", 0),), half)
    piece = lax.all_gather(amps, "col", axis=2, tiled=True)
    exact = lax.Precision.HIGHEST
    outs = []
    for s in range(slots):
        summed = integrals[:, :, :, s]
        for q in range(terms):
            inner = jnp.einsum("axy,aijyz->aijxz", ladder_factors[:, q], amps[:, :, :, s], precision=exact)
            summed = summed + jnp.einsum("aijxz,awz->aijxw", inner, factors[s : s + count, q], precision=exact)
        for t in range(slots):
            m = s - t + half
            if 0 <= m < slots:
                summed = summed + jnp.einsum(
                    "aiktu,akjuv->aijtv", piece[:, :, :, t], cycle_all[t : t + count, :, :, m], precision=exact
                )
        outs.append(summed)
    return keep_float * jnp.stack(outs, axis=3)


def solution(mesh):
    in_specs = (
        P("vir", "row", "col", None, None, None),
        P("vir", "row", "col", None, None, None),
        P("vir", "row", "col", None, None, None),
        P("vir", None, None, None),
        P("vir", "row", "col", None),
    )
    out_specs = P("vir", "row", "col", None, None, None)

    def run(amplitudes, *rest):
        tiles, first_pairs, second_pairs, slots = amplitudes.shape[:4]
        shape = dict(mesh.shape)
        local = tiles // shape["vir"]
        fits = shape["row"] == shape["col"] == first_pairs == second_pairs == 4
        if fits and slots == 3 and local % 2 == 0:
            body = functools.partial(per_device, tiles, 6, 2)
        else:
            body = functools.partial(general, tiles)
        return jax.shard_map(body, mesh=mesh, in_specs=in_specs, out_specs=out_specs, check_vma=False)(
            amplitudes, *rest
        )

    return run
```
